32 devices in a mesh: seq: 8 (over z, x), ep: 4 (over y, core).
Axes of the slice: x: 2, y: 2, z: 4, core: 2. Of those that a mesh axis runs over, the one named last changes fastest.
Arguments:
- tokens: bfloat16 [1024, 2048], P('seq'), may hold values from -12 to 12
- attn_gain: float32 [2048], replicated, may hold values from 0.1 to 1.9
- w_query: bfloat16 [2048, 512], P(None, 'ep'), may hold values from -1 to 1
- w_key: bfloat16 [2048, 512], P(None, 'ep'), may hold values from -8 to 8
- w_value: bfloat16 [2048, 512], P(None, 'ep'), may hold values from -0.125 to 0.125
- w_out: bfloat16 [512, 2048], P('ep'), may hold values from -0.25 to 0.25
- moe_gain: float32 [2048], replicated, may hold values from 0.1 to 1.9
- expert_ids: int32 [1024, 6], P('seq'), may hold values from 0 to 15, all different within a row; in each aligned block of 128 rows (0 to 127, 128 to 255, ...) at most 52 rows name the same one
- route_weight: float32 [1024, 6], P('seq'), may hold values from 0.2 to 1
- w_gate: bfloat16 [5632, 2048], P(('seq', 'ep')), may hold values from -0.125 to 0.125
- w_up: bfloat16 [5632, 2048], P(('seq', 'ep')), may hold values from -0.125 to 0.125
- w_down: bfloat16 [5632, 2048], P(('seq', 'ep')), may hold values from -0.3125 to 0.3125
Outputs:
- layer_out: bfloat16 [1024, 2048], P(('seq', 'ep'))
The draws below stay inside these ranges and needn't reach their ends.
Inputs may be any that keep to these rules, and one draw needn't show every extreme that they name: `expert_ids`: each frame names 6 different experts; among the frames of one block of 128 no expert is named by more than 52 frames, a bound that some block reaches.
All inputs are finite; a program needn't handle non-finite values.
Results may differ from the reference program's by a relative error of at most 0.0065.
Values may be sent and summed in bfloat16 or wider, within the bound.
A program may use at most 64 MiB of HBM per device.

```python
import math
import jax
import jax.numpy as jnp
import numpy as np
from jax import lax

D = 2048
HEAD_WIDTH = 128
TOPK = 6
FF_DEV = 176
SPAN = 4
TOK_DEV = 128
SLICES = 2
FF = 352
EXPERTS = 16
HEADS = 4
TOKENS = 1024
WINDOW = 512
CAP = 52


def shared_query(key):
    return jax.random.normal(jax.random.fold_in(key, 101), (D, HEADS * HEAD_WIDTH), jnp.float32) * D ** (-0.5)


def draw_tokens(key, part):
    column_scale = jnp.exp(jax.random.uniform(jax.random.fold_in(key, 1), (D,), jnp.float32, math.log(0.3), math.log(3.0)))
    base = jax.random.normal(jax.random.fold_in(key, 2), (TOKENS, D), jnp.float32)
    values = base * column_scale
    return jnp.clip(values, -12.0, 12.0).astype(jnp.bfloat16)


def draw_w_query(key, part):
    return jnp.clip(shared_query(key), -1.0, 1.0).astype(jnp.bfloat16)


def draw_w_key(key, part):
    noise = jax.random.normal(jax.random.fold_in(key, 202), (D, HEADS * HEAD_WIDTH), jnp.float32) * D ** (-0.5)
    values = noise
    return jnp.clip(values, -8.0, 8.0).astype(jnp.bfloat16)


def steps_of(key, extent, shards, low, top_value):
    factor_of = 1.0
    for axis_at, blocks in shards:
        draws = jax.random.uniform(jax.random.fold_in(jax.random.fold_in(key, 6), axis_at), (blocks,), jnp.float32, low / len(shards), top_value / len(shards))
        factor_of = factor_of * jnp.repeat(jnp.exp(draws), extent[axis_at] // blocks).reshape((-1,) + (1,) * (len(extent) - 1 - axis_at))
    return factor_of


def routed_block(own_key, own, number, rows, amount, top, reach, skew):
    order = jax.random.permutation(own_key, amount)
    packed, ordinary = load_shares(amount, rows * top, reach, skew, True), load_shares(amount, rows * top, reach, skew, False)
    places = jnp.arange(amount)

    def named(lengths, turn):
        used = int((lengths > 0).sum())
        fixed = max(1, used // 4)
        passed = fixed + (places - fixed + turn * (used - fixed)) % max(1, amount - fixed)
        return jnp.zeros((amount,), jnp.int32).at[order[jnp.where(places < fixed, places, passed)]].set(jnp.asarray(lengths, jnp.int32))

    lengths = jnp.where(number % 4 == 0, named(packed, number // 4), named(ordinary, number - number // 4 - 1))
    mixed = jax.random.permutation(jax.random.fold_in(own, 3), amount)
    donor, taker = mixed[0:amount // 2 * 2:2], mixed[1:amount // 2 * 2:2]
    slack = jnp.minimum(lengths[donor] - 1, reach - lengths[taker]) // 2
    slack = jnp.where((donor == order[0]) | (taker == order[0]) | (lengths[taker] == 0), 0, jnp.maximum(slack, 0))
    passed = jax.random.randint(jax.random.fold_in(own, 4), (amount // 2,), 0, 1 << 20) % (slack + 1)
    lengths = lengths.at[donor].add(-passed).at[taker].add(passed)
    items = jnp.searchsorted(jnp.cumsum(lengths), jnp.arange(rows * top), side="right").astype(jnp.int32)
    grid = items.reshape(top, rows).T
    grid = grid[jax.random.permutation(jax.random.fold_in(own, 1), rows)]
    turn = jax.random.randint(jax.random.fold_in(own, 2), (rows, 1), 0, top)
    return jnp.take_along_axis(grid, (jnp.arange(top)[None, :] + turn) % top, axis=1)


def load_shares(count, total, limit, slope, full):
    weights = [(1 << 20) // math.isqrt(rank ** slope) + 1 for rank in range(1, count + 1)]
    largest = limit if full else min(limit, max(-(-total // count), total * weights[0] // sum(weights)))
    least = 1 if total - largest >= count - 1 else 0
    given, rest = [largest] + [least] * (count - 1), total - largest - least * (count - 1)
    while rest > 0:
        movable = [i for i in range(1, count) if given[i] < largest] or [i for i in range(1, count) if given[i] < limit]
        whole, budget = sum([weights[i] for i in movable]), rest
        for i in movable:
            addition = min(limit - given[i], max(1, budget * weights[i] // whole), rest)
            given[i] = given[i] + addition
            rest = rest - addition
    return np.array(given)


def centred(rng, extent, spread, bound, shards=(), kind=jnp.bfloat16):
    entries = spread * jax.random.normal(rng, extent, jnp.float32)
    if shards:
        entries = entries * steps_of(rng, extent, shards, -0.22, 0.18)
    return jnp.clip(entries, -bound, bound).astype(kind)


def setup_inputs(seed: int = 0) -> dict:
    arg_keys = jax.random.split(jax.random.key(seed), 13)
    tokens = draw_tokens(jax.random.fold_in(arg_keys[12], 71), 0)
    attn_gain = jnp.clip(1.0 + 0.18 * jax.random.normal(arg_keys[1], (D,), jnp.float32), 0.1, 1.9)
    w_query = draw_w_query(jax.random.fold_in(arg_keys[12], 71), 0)
    w_key = draw_w_key(jax.random.fold_in(arg_keys[12], 71), 0)
    w_value = centred(arg_keys[4], (D, HEADS * HEAD_WIDTH), D ** -0.5, 0.125, ((1, 4),))
    w_out = centred(arg_keys[5], (HEADS * HEAD_WIDTH, D), (HEADS * HEAD_WIDTH) ** -0.5, 0.25, ((0, 4),))
    moe_gain = jnp.clip(1.0 + 0.18 * jax.random.normal(arg_keys[6], (D,), jnp.float32), 0.1, 1.9)
    expert_ids_keys = jax.random.split(jax.random.fold_in(arg_keys[7], 1), TOKENS // TOK_DEV)
    expert_ids_turns = jax.random.permutation(jax.random.fold_in(arg_keys[7], 3), TOKENS // TOK_DEV)
    expert_ids = jax.vmap(lambda own, number: routed_block(jax.random.fold_in(arg_keys[7], 2), own, number, TOK_DEV, EXPERTS, TOPK, CAP, 2))(expert_ids_keys, expert_ids_turns).reshape((TOKENS, TOPK))
    route_weight = jnp.clip(0.2 + 0.8 * jax.random.uniform(arg_keys[8], (TOKENS, TOPK), jnp.float32) ** steps_of(arg_keys[8], (TOKENS, TOPK), ((0, 8),), -0.2, 0.2), 0.2, 1.0)
    w_gate = centred(arg_keys[9], (EXPERTS * FF, D), D ** -0.5, 0.125, ((0, 32),))
    w_up = centred(arg_keys[10], (EXPERTS * FF, D), D ** -0.5, 0.125, ((0, 32),))
    w_down = centred(arg_keys[11], (EXPERTS * FF, D), FF ** -0.5, 0.3125, ((0, 32),))
    return dict(tokens=tokens, attn_gain=attn_gain, w_query=w_query, w_key=w_key, w_value=w_value, w_out=w_out, moe_gain=moe_gain, expert_ids=expert_ids, route_weight=route_weight, w_gate=w_gate, w_up=w_up, w_down=w_down)


epsilon = 1e-05

def root_norm(values, gain):
    mean_square = lax.optimization_barrier(jnp.mean(values * values, axis=-1, keepdims=True))
    return values * lax.rsqrt(mean_square + epsilon) * gain

def reference(tokens, attn_gain, w_query, w_key, w_value, w_out, moe_gain, expert_ids, route_weight, w_gate, w_up, w_down):
    tok_float = tokens.astype(jnp.float32)
    normed = root_norm(tok_float, attn_gain).astype(jnp.bfloat16)
    blocks = TOKENS // TOK_DEV
    query_pos = jnp.arange(TOK_DEV, dtype=jnp.int32)[:, None]
    key_rel = jnp.arange((SPAN + 1) * TOK_DEV, dtype=jnp.int32)[None, :] - SPAN * TOK_DEV
    block_ids = jnp.arange(blocks, dtype=jnp.int32)[:, None, None]
    allowed = (key_rel <= query_pos) & (key_rel > query_pos - WINDOW)
    allowed = allowed[None] & (block_ids * TOK_DEV + key_rel[None] >= 0)

    def project(weight, start):
        columns = lax.dynamic_slice_in_dim(weight, start, HEAD_WIDTH, 1)
        result = jnp.dot(normed, columns, preferred_element_type=jnp.float32).astype(jnp.bfloat16)
        return result.reshape(blocks, TOK_DEV, HEAD_WIDTH)

    def with_previous(current):
        pieces = []
        for distance in range(SPAN, 0, -1):
            zero_blocks = jnp.zeros((distance, TOK_DEV, HEAD_WIDTH), jnp.bfloat16)
            pieces.append(jnp.concatenate([zero_blocks, current[:blocks - distance]], axis=0))
        pieces.append(current)
        return jnp.concatenate(pieces, axis=1)

    def head_step(total, head_index):
        start = head_index * HEAD_WIDTH
        query_vectors = project(w_query, start)
        window_key_rows = with_previous(project(w_key, start))
        window_value_rows = with_previous(project(w_value, start))
        attention_logits = jnp.einsum('muo,mgo->mug', query_vectors.astype(jnp.float32), window_key_rows.astype(jnp.float32)) / math.sqrt(HEAD_WIDTH)
        attention_logits = jnp.where(allowed, attention_logits, -1e+30)
        peak = lax.optimization_barrier(jnp.max(attention_logits, axis=-1, keepdims=True))
        expo = jnp.exp(attention_logits - peak)
        attention_probabilities = (expo / lax.optimization_barrier(jnp.sum(expo, axis=-1, keepdims=True))).astype(jnp.bfloat16)
        attention_output = jnp.einsum('hwa,ham->hwm', attention_probabilities.astype(jnp.float32), window_value_rows.astype(jnp.float32))
        attention_output = attention_output.astype(jnp.bfloat16).reshape(TOKENS, HEAD_WIDTH)
        out_rows = lax.dynamic_slice_in_dim(w_out, start, HEAD_WIDTH, 0)
        return (total + jnp.dot(attention_output, out_rows, preferred_element_type=jnp.float32), None)
    attn_total = lax.scan(head_step, jnp.zeros((TOKENS, D), jnp.float32), jnp.arange(HEADS, dtype=jnp.int32))[0]
    residual = tok_float + attn_total
    moe_in = root_norm(residual, moe_gain).astype(jnp.bfloat16)
    expert_iota = jnp.arange(EXPERTS, dtype=jnp.int32)
    chosen = (expert_ids[:, :, None] == expert_iota).astype(jnp.int32)
    counts = lax.optimization_barrier(jnp.sum(chosen, axis=1)).reshape(blocks, TOK_DEV, EXPERTS)
    before = (jnp.cumsum(counts, axis=1) - counts).reshape(TOKENS, EXPERTS)
    slot_index = lax.optimization_barrier(jnp.sum(chosen * before[:, None, :], axis=-1)).astype(jnp.int32)
    block_of = (jnp.arange(TOKENS, dtype=jnp.int32) // TOK_DEV)[:, None]
    column = (block_of * CAP + slot_index).astype(jnp.int32)
    token_of = jnp.broadcast_to(jnp.arange(TOKENS, dtype=jnp.int32)[:, None], expert_ids.shape)
    table = jnp.zeros((EXPERTS, blocks * CAP), jnp.int32).at[expert_ids.reshape(-1), column.reshape(-1)].set(token_of.reshape(-1))
    filled = jnp.zeros((EXPERTS, blocks * CAP), jnp.float32).at[expert_ids.reshape(-1), column.reshape(-1)].set(1.0)

    def expert_step(expert):
        panel = moe_in[table[expert]] * filled[expert][:, None].astype(jnp.bfloat16)
        gate_rows = lax.dynamic_slice_in_dim(w_gate, expert * FF, FF, 0)
        up_rows = lax.dynamic_slice_in_dim(w_up, expert * FF, FF, 0)
        down_rows = lax.dynamic_slice_in_dim(w_down, expert * FF, FF, 0)
        gate = jnp.dot(panel, gate_rows.T, preferred_element_type=jnp.float32)
        upward = jnp.dot(panel, up_rows.T, preferred_element_type=jnp.float32)
        hidden = (jax.nn.silu(gate) * upward).astype(jnp.bfloat16)
        sliced = jnp.einsum('rsf,sfd->srd', hidden.astype(jnp.float32).reshape(-1, SLICES, FF_DEV), down_rows.astype(jnp.float32).reshape(SLICES, FF_DEV, D))
        rounded = lax.optimization_barrier(sliced.astype(jnp.bfloat16))
        return lax.optimization_barrier(jnp.sum(rounded.astype(jnp.float32), axis=0))
    expert_rows = lax.map(expert_step, expert_iota)
    pair_out = expert_rows[expert_ids, column]
    rate = lax.optimization_barrier(route_weight.astype(jnp.bfloat16)).astype(jnp.float32)
    moe = lax.optimization_barrier(jnp.sum(rate[:, :, None] * pair_out, axis=1))
    return (residual + moe).astype(jnp.bfloat16)
```

```python
import functools
import math

import jax
import jax.numpy as jnp
from jax import lax
from jax.experimental import pallas as pl
from jax.experimental.pallas import tpu as pltpu
from jax.sharding import PartitionSpec as P

EXP_ROW = 2
SPAN = 4
EPS = 1e-05
F32 = jnp.float32
BF16 = jnp.bfloat16
MESH = pl.DeviceIdType.MESH


def dot(a, b, dims=((1,), (0,))):
    return lax.dot_general(a, b, (dims, ((), ())), preferred_element_type=F32)


def kernel(
    S,
    E,
    cap,
    slots,
    tokens,
    attn_gain,
    w_query,
    w_key,
    w_value,
    w_out,
    moe_gain,
    ids_ref,
    route_ref,
    w_gate,
    w_up,
    w_down,
    out_ref,
    kv,
    wout,
    att,
    squares,
    squares_in,
    panels,
    arrived,
    passed,
    gate_w,
    up_w,
    down_w,
    halves,
    halves_in,
    summed,
    returned,
    part_far,
    part_near,
    far_in,
    near_in,
    wout_send,
    wout_recv,
    kv_send,
    kv_recv,
    att_send,
    att_recv,
    sq_sem,
    disp_send,
    disp_recv,
    pass_send,
    pass_recv,
    half_send,
    half_recv,
    ret_send,
    ret_recv,
    fin_send,
    fin_recv,
    load_sem,
):
    rows, width = tokens.shape
    head = w_query.shape[1]
    half = width // 2
    share = rows // E
    s = lax.axis_index("seq")
    e = lax.axis_index("ep")
    c = lax.rem(e, 2)
    mate = e + 1 - 2 * c
    own_cols = pl.ds(pl.multiple_of(c * half, 128), half)
    mate_cols = pl.ds(pl.multiple_of((1 - c) * half, 128), half)
    seq_peer = [lax.rem(s + r, S) for r in range(S)]
    ep_peer = [lax.rem(e + r, E) for r in range(E)]

    def remote(src, dst, send, recv, seq=None, ep=None):
        return pltpu.make_async_remote_copy(
            src_ref=src,
            dst_ref=dst,
            send_sem=send,
            recv_sem=recv,
            device_id=(s if seq is None else seq, e if ep is None else ep),
            device_id_type=MESH,
        )

    barrier = pltpu.get_barrier_semaphore()
    for r in range(1, S):
        pl.semaphore_signal(barrier, inc=1, device_id=(seq_peer[r], e), device_id_type=MESH)
    for r in range(1, E):
        pl.semaphore_signal(barrier, inc=1, device_id=(s, ep_peer[r]), device_id_type=MESH)

    loads = [
        pltpu.make_async_copy(w_gate, gate_w, load_sem.at[0]),
        pltpu.make_async_copy(w_up, up_w, load_sem.at[1]),
        pltpu.make_async_copy(w_down, down_w, load_sem.at[2]),
        pltpu.make_async_copy(
            w_out.at[:, own_cols],
            wout.at[pl.ds(pl.multiple_of(e * head, 128), head), :],
            load_sem.at[3],
        ),
    ]
    for copy in loads:
        copy.start()

    normed = tokens[...].astype(F32)
    mean_square = jnp.mean(normed * normed, axis=-1, keepdims=True)
    normed = (normed * lax.rsqrt(mean_square + EPS) * attn_gain[...]).astype(BF16)
    own_rows = pl.ds(SPAN * rows, rows)
    kv[own_rows, :head] = dot(normed, w_key[...]).astype(BF16)
    kv[own_rows, head:] = dot(normed, w_value[...]).astype(BF16)

    pl.semaphore_wait(barrier, S - 1 + E - 1)

    kv_copies = {}
    for d in range(1, SPAN + 1):
        kv_copies[d] = remote(
            kv.at[own_rows, :],
            kv.at[pl.ds((SPAN - d) * rows, rows), :],
            kv_send.at[d],
            kv_recv.at[d],
            seq=lax.rem(s + d, S),
        )

        @pl.when(s + d < S)
        def _(d=d):
            kv_copies[d].start()

    wout_copies = {}
    for r in range(1, E):
        peer = ep_peer[r]
        cols = pl.ds(pl.multiple_of(lax.rem(peer, 2) * half, 128), half)
        wout_copies[r] = remote(
            w_out.at[:, cols],
            wout.at[pl.ds(pl.multiple_of(e * head, 128), head), :],
            wout_send.at[r],
            wout_recv.at[r],
            ep=peer,
        )
        wout_copies[r].start()

    query = dot(normed, w_query[...]).astype(BF16)

    expert_half = e // (E // EXP_ROW)
    lane = lax.broadcasted_iota(jnp.int32, (rows, 128), 1)
    ids = ids_ref[...]
    rate = route_ref[...].astype(BF16).astype(F32)
    chosen = jnp.zeros((rows, 128), F32)
    rates = jnp.zeros((rows, 128), F32)
    for k in range(ids.shape[1]):
        hit = (ids[:, k : k + 1] == lane * EXP_ROW + expert_half) & (lane < S)
        chosen = jnp.where(hit, 1.0, chosen)
        rates = jnp.where(hit, rate[:, k : k + 1], rates)
    earlier = (
        lax.broadcasted_iota(jnp.int32, (rows, rows), 0)
        > lax.broadcasted_iota(jnp.int32, (rows, rows), 1)
    ).astype(F32)
    before = dot(earlier.astype(BF16), chosen.astype(BF16))
    place = jnp.where(chosen > 0.5, before, 255.0).astype(BF16)
    spread_row = lax.broadcasted_iota(jnp.int32, (128, S * slots), 0) * slots
    spread_lane = lax.broadcasted_iota(jnp.int32, (128, S * slots), 1)
    spread = jnp.where(
        (spread_lane >= spread_row) & (spread_lane < spread_row + slots), 1.0, 0.0
    ).astype(BF16)
    slot_of = (lax.broadcasted_iota(jnp.int32, (rows, S * slots), 1) % slots).astype(F32)
    filled = dot(place, spread) == slot_of
    dispatch = jnp.where(filled, 1.0, 0.0).astype(BF16)
    combine = jnp.where(filled, dot(rates.astype(BF16), spread), 0.0).astype(BF16)

    for d in range(1, SPAN + 1):

        @pl.when(s < d)
        def _(d=d):
            kv[pl.ds((SPAN - d) * rows, rows), :] = jnp.zeros((rows, 2 * head), BF16)

    for d in range(1, SPAN + 1):

        @pl.when(s >= d)
        def _(d=d):
            kv_copies[d].wait_recv()

    window = SPAN * rows
    logits = dot(query, kv[:, :head], ((1,), (1,))) / math.sqrt(head)
    query_pos = lax.broadcasted_iota(jnp.int32, logits.shape, 0)
    key_rel = lax.broadcasted_iota(jnp.int32, logits.shape, 1) - window
    allowed = (
        (key_rel <= query_pos) & (key_rel > query_pos - window) & (s * rows + key_rel >= 0)
    )
    logits = jnp.where(allowed, logits, -1e30)
    expo = jnp.exp(logits - jnp.max(logits, axis=-1, keepdims=True))
    probs = (expo / jnp.sum(expo, axis=-1, keepdims=True)).astype(BF16)
    own_head = pl.ds(pl.multiple_of(e * head, 128), head)
    att[:, own_head] = dot(probs, kv[:, head:]).astype(BF16)

    att_copies = {}
    for r in range(1, E):
        att_copies[r] = remote(
            att.at[:, own_head], att.at[:, own_head], att_send.at[r], att_recv.at[r], ep=ep_peer[r]
        )
        att_copies[r].start()
    loads[3].wait()
    for r in range(1, E):
        wout_copies[r].wait_recv()
    for r in range(1, E):
        att_copies[r].wait_recv()

    residual = tokens[:, own_cols].astype(F32) + dot(att[...], wout[...])
    partial = jnp.zeros((rows, 128), F32)
    for i in range(half // 128):
        piece = residual[:, i * 128 : (i + 1) * 128]
        partial = partial + piece * piece
    squares[...] = partial
    sq_copy = remote(squares, squares_in, sq_sem.at[0], sq_sem.at[1], ep=mate)
    sq_copy.start()
    sq_copy.wait_recv()
    mean_square = jnp.sum(partial + squares_in[...], axis=-1, keepdims=True) / width
    moe_in = (residual * lax.rsqrt(mean_square + EPS) * moe_gain[:, own_cols]).astype(BF16)
    panels[...] = (
        dot(dispatch, moe_in, ((0,), (0,))).reshape(S, slots, half).astype(BF16)
    )

    disp = {}
    for r in range(1, S):
        disp[r] = remote(
            panels.at[seq_peer[r]], arrived.at[s], disp_send.at[r], disp_recv.at[r], seq=seq_peer[r]
        )
        disp[r].start()
    arrived[s] = panels[s]

    passes = {}
    for r in range(S):
        source = lax.rem(s + S - r, S)
        if r:
            disp[r].wait_recv()
        passes[r] = remote(
            arrived.at[source], passed.at[source], pass_send.at[r], pass_recv.at[r], ep=mate
        )
        passes[r].start()
    for copy in loads[:3]:
        copy.wait()
    mine = arrived[...].astype(F32).reshape(S * slots, half).astype(BF16)
    gate = dot(mine, gate_w[:, own_cols], ((1,), (1,)))
    upward = dot(mine, up_w[:, own_cols], ((1,), (1,)))
    for r in range(S):
        passes[r].wait_recv()
    others = passed[...].astype(F32).reshape(S * slots, half).astype(BF16)
    gate = gate + dot(others, gate_w[:, mate_cols], ((1,), (1,)))
    upward = upward + dot(others, up_w[:, mate_cols], ((1,), (1,)))
    hidden = (gate / (1.0 + jnp.exp(-gate)) * upward).astype(BF16)

    halves[...] = dot(hidden, down_w[:, mate_cols]).reshape(S, slots, half).astype(BF16)
    half_copies = {}
    for r in range(S):
        half_copies[r] = remote(
            halves.at[seq_peer[r]],
            halves_in.at[seq_peer[r]],
            half_send.at[r],
            half_recv.at[r],
            ep=mate,
        )
        half_copies[r].start()
    result = dot(hidden, down_w[:, own_cols]).reshape(S, slots, half)
    for r in range(S):
        half_copies[r].wait_recv()
    summed[...] = (result + halves_in[...].astype(F32)).astype(BF16)
    ret = {}
    for r in range(1, S):
        ret[r] = remote(
            summed.at[seq_peer[r]], returned.at[s], ret_send.at[r], ret_recv.at[r], seq=seq_peer[r]
        )
        ret[r].start()
    returned[s] = summed[s]
    for r in range(1, S):
        ret[r].wait_recv()

    moe = dot(combine, returned[...].astype(F32).reshape(S * slots, half).astype(BF16))
    part_far[...] = moe.reshape(E, share, half).astype(BF16)
    part_near[...] = (moe + residual).reshape(E, share, half)
    fin_near = remote(
        part_near.at[mate], near_in, fin_send.at[0], fin_recv.at[0], ep=mate
    )
    fin_near.start()
    pair = e // 2
    fin_far = {}
    for r in range(1, E // 2):
        for other in range(2):
            peer = 2 * lax.rem(pair + r, E // 2) + other
            at = 2 * r + other
            fin_far[at] = remote(
                part_far.at[peer],
                far_in.at[r - 1, c],
                fin_send.at[at],
                fin_recv.at[2 * r + c],
                ep=peer,
            )
            fin_far[at].start()
    own = part_near[e]
    fin_near.wait_recv()
    near = near_in[...]
    sides = [jnp.where(c == 0, own, near), jnp.where(c == 0, near, own)]
    for r in range(1, E // 2):
        for other in range(2):
            arrival = remote(
                part_far.at[e],
                far_in.at[r - 1, other],
                fin_send.at[2 * r + other],
                fin_recv.at[2 * r + other],
                ep=mate,
            )
            arrival.wait_recv()
            sides[other] = sides[other] + far_in[r - 1, other].astype(F32)
    out_ref[:, :half] = sides[0].astype(BF16)
    out_ref[:, half:] = sides[1].astype(BF16)

    for d in range(1, SPAN + 1):

        @pl.when(s + d < S)
        def _(d=d):
            kv_copies[d].wait_send()

    sends = [sq_copy, fin_near]
    for group in (wout_copies, att_copies, disp, passes, half_copies, ret, fin_far):
        sends += list(group.values())
    for copy in sends:
        copy.wait_send()


def body(
    tokens,
    attn_gain,
    w_query,
    w_key,
    w_value,
    w_out,
    moe_gain,
    expert_ids,
    route_weight,
    w_gate,
    w_up,
    w_down,
):
    rows, width = tokens.shape
    head = w_query.shape[1]
    S = lax.axis_size("seq")
    E = lax.axis_size("ep")
    half = width // 2
    share = rows // E
    ff = w_gate.shape[0]
    cap = rows * expert_ids.shape[1] // (S * EXP_ROW) + rows // 32
    slots = -(-cap // 8) * 8
    vmem = pl.BlockSpec(memory_space=pltpu.VMEM)
    hbm = pl.BlockSpec(memory_space=pl.ANY)
    panel = pltpu.VMEM((S, slots, half), BF16)
    dma = pltpu.SemaphoreType.DMA
    return pl.pallas_call(
        functools.partial(kernel, S, E, cap, slots),
        out_shape=jax.ShapeDtypeStruct((share, width), BF16),
        in_specs=[vmem, vmem, vmem, vmem, vmem, hbm, vmem, vmem, vmem, hbm, hbm, hbm],
        out_specs=vmem,
        scratch_shapes=[
            pltpu.VMEM(((SPAN + 1) * rows, 2 * head), BF16),
            pltpu.VMEM((E * head, half), BF16),
            pltpu.VMEM((rows, E * head), BF16),
            pltpu.VMEM((rows, 128), F32),
            pltpu.VMEM((rows, 128), F32),
            panel,
            panel,
            panel,
            pltpu.VMEM((ff, width), BF16),
            pltpu.VMEM((ff, width), BF16),
            pltpu.VMEM((ff, width), BF16),
            panel,
            panel,
            panel,
            panel,
            pltpu.VMEM((E, share, half), BF16),
            pltpu.VMEM((E, share, half), F32),
            pltpu.VMEM((E // 2 - 1, 2, share, half), BF16),
            pltpu.VMEM((share, half), F32),
            dma((E,)),
            dma((E,)),
            dma((SPAN + 1,)),
            dma((SPAN + 1,)),
            dma((E,)),
            dma((E,)),
            dma((2,)),
            dma((S,)),
            dma((S,)),
            dma((S,)),
            dma((S,)),
            dma((S,)),
            dma((S,)),
            dma((S,)),
            dma((S,)),
            dma((E,)),
            dma((E,)),
            dma((4,)),
        ],
        compiler_params=pltpu.CompilerParams(
            collective_id=0, has_side_effects=True, vmem_limit_bytes=56 * 1024 * 1024
        ),
    )(
        tokens,
        attn_gain.reshape(1, width),
        w_query,
        w_key,
        w_value,
        w_out,
        moe_gain.reshape(1, width),
        expert_ids,
        route_weight,
        w_gate,
        w_up,
        w_down,
    )


def solution(mesh):
    in_specs = (
        P("seq", None),
        P(),
        P(None, "ep"),
        P(None, "ep"),
        P(None, "ep"),
        P("ep", None),
        P(),
        P("seq", None),
        P("seq", None),
        P(("seq", "ep"), None),
        P(("seq", "ep"), None),
        P(("seq", "ep"), None),
    )
    out_specs = P(("seq", "ep"), None)
    return jax.shard_map(body, mesh=mesh, in_specs=in_specs, out_specs=out_specs, check_vma=False)
```
